1024 devices in a mesh: row: 128 (over x, y_hi, z), col: 8 (over y_lo, core).
Axes of the slice: x: 4, y: 8 (y_hi: 2, y_lo: 4; y = y_hi * 4 + y_lo), z: 16, core: 2. Of those that a mesh axis runs over, the one named last changes fastest.
Arguments:
- tokens: bfloat16 [256, 8192], P('row', 'col'), may hold values from -6 to 6
- out_grad: bfloat16 [256, 8192], P('row', 'col'), may hold values from -1.5 to 1.5
- in_weight: bfloat16 [128, 8, 128, 128], P('row', 'col'), may hold values from -0.1875 to 0.1875
- out_weight: bfloat16 [128, 8, 128, 128], P('row', 'col'), may hold values from -0.125 to 0.125
- in_blocks: int32 [128, 8], P(None, 'col'), may hold values from 0 to 63, as said below
- out_blocks: int32 [128, 8], P(None, 'col'), may hold values from 0 to 63, as said below
Outputs:
- mixed: bfloat16 [256, 8192], P('row', 'col')
- in_grad: bfloat16 [256, 8192], P('row', 'col')
- in_weight_grad: float32 [128, 8, 128, 128], P('row', 'col')
- out_weight_grad: float32 [128, 8, 128, 128], P('row', 'col')
The draws below stay inside these ranges and needn't reach their ends.
Inputs may be any that keep to these rules, and one draw needn't show every extreme that they name: `in_blocks`: each row j names 8 distinct feature blocks, 1 in each run of 8 blocks, runs in order along the row (entries k * 1 to (k + 1) - 1 lie in blocks k * 8 to (k + 1) * 8 - 1); inside a run the block's offset differs from j mod 8 in at most one bit. `out_blocks`: same structure as in_blocks, drawn independently.
All inputs are finite; a program needn't handle non-finite values.
Results may differ from the reference program's by a relative error of at most 0.0049.
Values may be sent and summed in bfloat16 or wider, within the bound.
No kernel may reach another device: no remote copies, remote signals or barrier semaphores. Data moves between devices by JAX's collectives and lax.ppermute only.
A program may use at most 32 MiB of HBM per device.

```python
import math
import jax
import jax.numpy as jnp

D = 8192
BLK = 128
KNZ = 8
FF_BLOCKS = 128
TOKENS = 256
SLICES = 8
SLICE_BLOCKS = 8
PER_SLICE = 1


def butterfly_blocks(key):
    hidden = jnp.arange(FF_BLOCKS, dtype=jnp.int32)[:, None, None]
    offset = jnp.arange(SLICE_BLOCKS, dtype=jnp.int32)[None, None, :]
    raw = jax.random.randint(key, (FF_BLOCKS, SLICES, SLICE_BLOCKS), 0, 65536, dtype=jnp.int32)
    differ = jnp.bitwise_xor(hidden % SLICE_BLOCKS, offset)
    near = (jnp.bitwise_and(differ, differ - 1) == 0).astype(jnp.int32)
    score = raw * SLICE_BLOCKS + offset + near * 4194304
    order = jnp.argsort(-score, axis=2)[:, :, :PER_SLICE].astype(jnp.int32)
    base = jnp.arange(SLICES, dtype=jnp.int32)[None, :, None] * SLICE_BLOCKS
    return (order + base).reshape(FF_BLOCKS, KNZ).astype(jnp.int32)


def draw_in_blocks(key, part):
    return butterfly_blocks(jax.random.fold_in(key, 11))


def draw_out_blocks(key, part):
    return butterfly_blocks(jax.random.fold_in(key, 23))


def shard_levels(own_key, shape, shards, smallest, high):
    level, own = 1.0, jax.random.fold_in(own_key, 6)
    for dim, shards_of in shards:
        heights = jnp.exp(jax.random.uniform(jax.random.fold_in(own, dim), (shards_of,), jnp.float32, smallest / len(shards), high / len(shards)))
        level = level * jnp.repeat(heights, shape[dim] // shards_of).reshape([-1 if axis == dim else 1 for axis in range(len(shape))])
    return level


def scatter_about(own_key, dims, width, bound, split=(), kind=jnp.bfloat16):
    gain = shard_levels(own_key, dims, split, -0.22, 0.18) if split else 1.0
    array = jax.random.normal(own_key, dims, jnp.float32) * width * gain
    return jnp.minimum(jnp.maximum(array, -bound), bound).astype(kind)


def setup_inputs(seed: int = 0) -> dict:
    seeds = jax.random.split(jax.random.key(seed), 7)
    return {
        "tokens": scatter_about(seeds[0], (TOKENS, D), 1.0, 6.0, ((0, 128), (1, 8))),
        "out_grad": scatter_about(seeds[1], (TOKENS, D), 0.25, 1.5, ((0, 128), (1, 8))),
        "in_weight": scatter_about(seeds[2], (FF_BLOCKS, KNZ, BLK, BLK), (KNZ * BLK) ** -0.5, 0.1875, ((0, 128), (1, 8))),
        "out_weight": scatter_about(seeds[3], (FF_BLOCKS, KNZ, BLK, BLK), (FF_BLOCKS * BLK // 8) ** -0.5, 0.125, ((0, 128), (1, 8))),
        "in_blocks": draw_in_blocks(jax.random.fold_in(seeds[6], 71), 0),
        "out_blocks": draw_out_blocks(jax.random.fold_in(seeds[6], 71), 0),
    }


def gelu_slope(value):
    cdf = 0.5 * (1.0 + jax.scipy.special.erf(value * (2.0 ** -0.5)))
    pdf = jnp.exp(-0.5 * value * value) * ((2.0 * math.pi) ** -0.5)
    return cdf + value * pdf


def reference(tokens, out_grad, in_weight, out_weight, in_blocks, out_blocks):
    count = D // BLK
    xblocks = tokens.reshape(TOKENS, count, BLK).astype(jnp.float32)
    dyblocks = out_grad.reshape(TOKENS, count, BLK).astype(jnp.float32)
    picked_x = xblocks[:, in_blocks]
    picked_dy = dyblocks[:, out_blocks]
    first_w = in_weight.astype(jnp.float32)
    second_w = out_weight.astype(jnp.float32)
    hidden = jnp.einsum('tjkb,jkbo->tjo', picked_x, first_w)
    active = jax.nn.gelu(hidden, approximate=False).astype(jnp.bfloat16)
    active_f = active.astype(jnp.float32)
    terms = jnp.einsum('tji,jkio->tjko', active_f, second_w)
    placed = jnp.zeros((TOKENS, count, BLK), jnp.float32).at[:, out_blocks].add(terms)
    mixed = placed.reshape(TOKENS, D).astype(jnp.bfloat16)
    hidden_grad = jnp.einsum('tjko,jkio->tji', picked_dy, second_w)
    pre_grad = (hidden_grad * gelu_slope(hidden)).astype(jnp.bfloat16)
    pre_f = pre_grad.astype(jnp.float32)
    out_weight_grad = jnp.einsum('tji,tjko->jkio', active_f, picked_dy)
    in_weight_grad = jnp.einsum('tjkb,tjo->jkbo', picked_x, pre_f)
    back_terms = jnp.einsum('tjo,jkbo->tjkb', pre_f, first_w)
    back_placed = jnp.zeros((TOKENS, count, BLK), jnp.float32).at[:, in_blocks].add(back_terms)
    in_grad = back_placed.reshape(TOKENS, D).astype(jnp.bfloat16)
    return (mixed, in_grad, in_weight_grad, out_weight_grad)
```

```python
import math

import jax
import jax.numpy as jnp
from jax import lax
from jax.sharding import PartitionSpec as P


def gelu_slope(value):
    cdf = 0.5 * (1.0 + jax.scipy.special.erf(value * 2.0 ** (-0.5)))
    pdf = jnp.exp(-0.5 * value * value) * (2.0 * math.pi) ** (-0.5)
    return cdf + value * pdf


def body(tokens, out_grad, in_weight, out_weight, in_blocks, out_blocks):
    row_count = lax.axis_size("row")
    width = in_weight.shape[2]
    slots = tokens.shape[1] // width
    local_rows = tokens.shape[0]
    total = local_rows * row_count
    every_in = in_blocks[:, 0] % slots
    every_out = out_blocks[:, 0] % slots
    w_in = in_weight[0, 0]
    w_out = out_weight[0, 0]
    x3 = tokens.reshape(local_rows, slots, width)
    dy3 = out_grad.reshape(local_rows, slots, width)
    send = jnp.stack([x3[:, every_in], dy3[:, every_out]], axis=0)
    send = send.transpose(2, 0, 1, 3).reshape(row_count * 2 * local_rows, width)
    got = lax.all_to_all(send, "row", 0, 0, tiled=True)
    got = got.reshape(row_count, 2, local_rows, width)
    picked_x = got[:, 0].reshape(total, width)
    picked_dy = got[:, 1].reshape(total, width)
    parts = jnp.stack(
        [
            jnp.dot(picked_x, w_in, preferred_element_type=jnp.float32),
            lax.dot_general(
                picked_dy, w_out, (((1,), (1,)), ((), ())), preferred_element_type=jnp.float32
            ),
        ],
        axis=0,
    )
    sums = lax.psum(parts, "col")
    hidden = sums[0]
    hidden_grad = sums[1]
    active = jax.nn.gelu(hidden, approximate=False).astype(jnp.bfloat16)
    pre_grad = (hidden_grad * gelu_slope(hidden)).astype(jnp.bfloat16)
    mixed_terms = jnp.dot(active, w_out, preferred_element_type=jnp.float32)
    in_terms = lax.dot_general(
        pre_grad, w_in, (((1,), (1,)), ((), ())), preferred_element_type=jnp.float32
    )
    back = jnp.stack([mixed_terms, in_terms], axis=1).reshape(total * 2, width)
    back = lax.all_to_all(back, "row", 0, 0, tiled=True)
    back = back.reshape(row_count, local_rows, 2, width)
    slot_ids = jnp.arange(slots, dtype=jnp.int32)
    out_table = (every_out[:, None] == slot_ids[None, :]).astype(jnp.float32)
    in_table = (every_in[:, None] == slot_ids[None, :]).astype(jnp.float32)
    mixed = jnp.einsum(
        "jb,jtf->tbf", out_table, back[:, :, 0], precision=lax.Precision.HIGHEST
    ).reshape(local_rows, slots * width)
    in_grad = jnp.einsum(
        "jb,jtf->tbf", in_table, back[:, :, 1], precision=lax.Precision.HIGHEST
    ).reshape(local_rows, slots * width)
    out_weight_grad = lax.dot_general(
        active, picked_dy, (((0,), (0,)), ((), ())), preferred_element_type=jnp.float32
    )
    in_weight_grad = lax.dot_general(
        picked_x, pre_grad, (((0,), (0,)), ((), ())), preferred_element_type=jnp.float32
    )
    return (
        mixed.astype(jnp.bfloat16),
        in_grad.astype(jnp.bfloat16),
        in_weight_grad[None, None],
        out_weight_grad[None, None],
    )


def solution(mesh):
    placed = (
        P("row", "col"),
        P("row", "col"),
        P("row", "col", None, None),
        P("row", "col", None, None),
        P(None, "col"),
        P(None, "col"),
    )
    return jax.shard_map(
        body,
        mesh=mesh,
        in_specs=placed,
        out_specs=(
            P("row", "col"),
            P("row", "col"),
            P("row", "col", None, None),
            P("row", "col", None, None),
        ),
        check_vma=False,
    )
```
